32 devices in a mesh: sx: 16 (over z, y, x), sy: 2 (over core).
Axes of the slice: x: 2, y: 2, z: 4, core: 2. Of those that a mesh axis runs over, the one named last changes fastest.
Arguments:
- snapshots: bfloat16 [1024, 3, 32, 256], P(None, None, 'sx', 'sy'), may hold values from -6 to 6
- quad_weight: float32 [3, 32, 256], P(None, 'sx', 'sy'), may hold values from 0.5 to 1200
- mode_guess: float32 [16, 64, 2, 8], replicated, may hold values from -6 to 6
- bins: int32 [16], replicated, may hold values from 1 to 127
- starts: int32 [64], replicated, may hold values from 0 to 768
Outputs:
- modes: float32 [16, 2, 8, 3, 32, 256], P(None, None, None, None, 'sx', 'sy')
- energy: float32 [16, 8], replicated
The draws below stay inside these ranges and needn't reach their ends.
All inputs are finite; a program needn't handle non-finite values.
Results may differ from the reference program's by a relative error of at most 0.0024.
Values may be sent and summed in bfloat16 or wider, within the bound.
A program may use at most 64 MiB of HBM per device.

```python
import math
import jax
import jax.numpy as jnp
from jax import lax

NFFT = 256
NB = 64
NF = 16
NM = 8
TT = 1024
CX = 2
CY = 128
NSX = 32
NSY = 256


def draw_quad_weight(key, part):
    key_base = jax.random.fold_in(key, 11)
    key_tile = jax.random.fold_in(key, 12)
    key_heavy = jax.random.fold_in(key, 13)
    base = jnp.exp(jax.random.uniform(key_base, (3, NSX, NSY), jnp.float32, math.log(0.5), math.log(4.0)))
    tiles_x = NSX // CX
    tiles_y = NSY // CY
    ntiles = tiles_x * tiles_y
    tile_factor = jnp.exp(jax.random.uniform(key_tile, (ntiles,), jnp.float32, 0.0, math.log(10.0)))
    heavy = jax.random.permutation(key_heavy, ntiles)[:2]
    tile_factor = tile_factor.at[heavy].set(300.0)
    row_tile = jnp.arange(NSX, dtype=jnp.int32) // CX
    col_tile = jnp.arange(NSY, dtype=jnp.int32) // CY
    tile_ids = row_tile[:, None] * tiles_y + col_tile[None, :]
    factor = tile_factor[tile_ids]
    return base * factor[None]


def set_ends(values, own_key, low, largest):
    longest = values.shape.index(max(values.shape))
    spots = []
    for shift in (0, 1):
        where = [jax.random.randint(jax.random.fold_in(own_key, axis), (), 0, length) for axis, length in enumerate(values.shape)]
        where[longest] = (where[longest] + shift) % values.shape[longest]
        spots.append(tuple(where))
    return values.at[spots[0]].set(low).at[spots[1]].set(largest)


def levels(own_key, extent, split, low, high):
    level = 1.0
    for dim, blocks in split:
        steps = jax.random.uniform(jax.random.fold_in(jax.random.fold_in(own_key, 6), dim), (blocks,), jnp.float32, low / len(split), high / len(split))
        level = level * jnp.repeat(jnp.exp(steps), extent[dim] // blocks).reshape((-1,) + (1,) * (len(extent) - 1 - dim))
    return level


def scatter_about(stream_key, shape, deviation, most, cuts=(), held_as=jnp.bfloat16):
    drawn = deviation * jax.random.normal(stream_key, shape, jnp.float32)
    if cuts:
        drawn = drawn * levels(stream_key, shape, cuts, -0.22, 0.18)
    return jnp.clip(drawn, -most, most).astype(held_as)


def setup_inputs(seed: int = 0) -> dict:
    keys = jax.random.split(jax.random.key(seed), 6)
    snapshots = scatter_about(keys[0], (TT, 3, NSX, NSY), 1.0, 6.0, ((2, 16), (3, 2)))
    quad_weight = draw_quad_weight(jax.random.fold_in(keys[5], 71), 0)
    mode_guess = scatter_about(keys[2], (NF, NB, 2, NM), 1.0, 6.0, (), jnp.float32)
    bins = set_ends(jax.random.randint(keys[3], (NF,), 1, NFFT // 2), jax.random.fold_in(keys[3], 1), 1, (NFFT // 2) - 1).astype(jnp.int32)
    starts = set_ends(jax.random.randint(keys[4], (NB,), 0, TT - NFFT + 1), jax.random.fold_in(keys[4], 1), 0, TT - NFFT).astype(jnp.int32)
    return {"snapshots": snapshots, "quad_weight": quad_weight, "mode_guess": mode_guess, "bins": bins, "starts": starts}


EPS = 1e-06

def make_twiddle(bins):
    steps = jnp.arange(NFFT, dtype=jnp.int32)
    window = 0.5 - 0.5 * jnp.cos(2.0 * jnp.pi * steps.astype(jnp.float32) / NFFT)
    norm_c = 1.0 / jnp.sqrt(jnp.sum(window * window))
    phase = bins[:, None] * steps[None, :] % NFFT
    angle = 2.0 * jnp.pi * phase.astype(jnp.float32) / NFFT
    twid = jnp.stack([norm_c * window * jnp.cos(angle), -(norm_c * window) * jnp.sin(angle)], axis=1)
    return twid.astype(jnp.bfloat16)

def weighted_slice(snapshots, quad_weight, twid, scale, starts, index):
    piece = lax.dynamic_index_in_dim(snapshots, index, 2, keepdims=False)
    times = starts[:, None] + jnp.arange(NFFT, dtype=jnp.int32)[None, :]
    windows = jnp.take(piece, times, axis=0)
    qhat = jnp.einsum('fpt,btvy->fpbvy', twid.astype(jnp.float32), windows.astype(jnp.float32))
    wslice = lax.dynamic_index_in_dim(quad_weight, index, 1, keepdims=False)
    colscale = scale[:, None] * jnp.sqrt(wslice)
    ydata = (qhat * colscale[None, None, None]).astype(jnp.bfloat16)
    return ydata.reshape(NF, 2 * NB, 3 * NSY)

def reference(snapshots, quad_weight, mode_guess, bins, starts):
    twid = make_twiddle(bins)

    def square_step(total, index):
        piece = lax.dynamic_index_in_dim(snapshots, index, 2, keepdims=False).astype(jnp.float32)
        wslice = lax.dynamic_index_in_dim(quad_weight, index, 1, keepdims=False)
        return (total + lax.optimization_barrier(jnp.sum(piece * piece * wslice[None], axis=(0, 2))), None)
    sums, _ = lax.scan(square_step, jnp.zeros((3,), jnp.float32), jnp.arange(NSX, dtype=jnp.int32))
    msq = sums / (TT * NSX * NSY)
    scale = lax.rsqrt(msq + EPS)

    def gram_step(total, index):
        ydata = weighted_slice(snapshots, quad_weight, twid, scale, starts, index).astype(jnp.float32)
        return (total + jnp.einsum('fax,fbx->fab', ydata, ydata), None)
    gram, _ = lax.scan(gram_step, jnp.zeros((NF, 2 * NB, 2 * NB), jnp.float32), jnp.arange(NSX, dtype=jnp.int32))
    gram_re = gram[:, :NB, :NB] + gram[:, NB:, NB:]
    gram_im = gram[:, :NB, NB:] - gram[:, NB:, :NB]
    denom = 3.0 * NSX * NSY
    gram_re = gram_re / denom
    gram_im = gram_im / denom
    hp = lax.Precision.HIGHEST
    guess_re = mode_guess[:, :, 0, :]
    guess_im = mode_guess[:, :, 1, :]
    zre = jnp.einsum('fbc,fcn->fbn', gram_re, guess_re, precision=hp) - jnp.einsum('fbc,fcn->fbn', gram_im, guess_im, precision=hp)
    zim = jnp.einsum('fbc,fcn->fbn', gram_re, guess_im, precision=hp) + jnp.einsum('fbc,fcn->fbn', gram_im, guess_re, precision=hp)
    norms = lax.optimization_barrier(jnp.sum(zre * zre + zim * zim, axis=1))
    energy = jnp.sqrt(norms / NB)
    inv = lax.rsqrt(norms + EPS)[:, None, :]
    coef_re = (zre * inv).astype(jnp.bfloat16)
    coef_im = (zim * inv).astype(jnp.bfloat16)
    upper = jnp.concatenate([coef_re, coef_im], axis=-1)
    lower = jnp.concatenate([-coef_im, coef_re], axis=-1)
    stacked = jnp.concatenate([upper, lower], axis=1).astype(jnp.float32)

    def mode_step(index):
        ydata = weighted_slice(snapshots, quad_weight, twid, scale, starts, index).astype(jnp.float32)
        return jnp.einsum('fan,fax->fnx', stacked, ydata).reshape(NF, 2, NM, 3, NSY)
    slices = lax.map(mode_step, jnp.arange(NSX, dtype=jnp.int32))
    modes = jnp.transpose(slices, (1, 2, 3, 4, 0, 5))
    return (modes, energy)
```

```python
import functools
import jax
import jax.numpy as jnp
from jax import lax
from jax.experimental import pallas as pl
from jax.experimental.pallas import tpu as pltpu
from jax.sharding import PartitionSpec as P

NFFT = 256
LANES = 128
EPS = 1e-06
MESH = pl.DeviceIdType.MESH


def make_twiddle(bins):
    steps = jnp.arange(NFFT, dtype=jnp.int32)
    window = 0.5 - 0.5 * jnp.cos(2.0 * jnp.pi * steps.astype(jnp.float32) / NFFT)
    norm_c = 1.0 / jnp.sqrt(jnp.sum(window * window))
    phase = bins[:, None] * steps[None, :] % NFFT
    angle = 2.0 * jnp.pi * phase.astype(jnp.float32) / NFFT
    twid = jnp.stack(
        [norm_c * window * jnp.cos(angle), -(norm_c * window) * jnp.sin(angle)], axis=1
    )
    return twid.astype(jnp.bfloat16)


def prep_kernel(dims, starts, x_ref, quad_ref, twid_ref, t_ref, xr_ref, sq_ref, xs):
    length, nvar, ctile, nblock, nq = dims
    rows = x_ref.shape[0]
    step = rows // 16

    @pl.loop(0, 16)
    def _(i):
        at = pl.ds(pl.multiple_of(i * step, step), step)
        xs[at, :] = x_ref[at, :].astype(jnp.float32)

    lane = lax.broadcasted_iota(jnp.int32, (1, LANES), 1)
    per_var = ctile // nvar
    total = jnp.zeros((1, LANES), jnp.float32)
    for c in range(ctile):
        col = xs[pl.ds(c, length, stride=ctile), :]
        xr_ref[:, c * LANES:(c + 1) * LANES] = col.astype(jnp.bfloat16)
        sums = jnp.sum(col * col, axis=0, keepdims=True) * quad_ref[c:c + 1, :]
        one = jnp.sum(sums, axis=1, keepdims=True)
        total = total + jnp.where(lane == c // per_var, one, 0.0)
    sq_ref[...] = total

    t_ref[...] = jnp.zeros_like(t_ref)
    tiles = NFFT // LANES
    wide = lax.broadcasted_iota(jnp.int32, (nq, LANES), 1)

    @pl.loop(0, nblock)
    def _(b):
        start = starts[b]
        tile = start // LANES
        shift = start - tile * LANES
        keep = wide < shift
        prev = jnp.zeros((nq, LANES), jnp.float32)
        outs = []
        for j in range(tiles):
            cur = pltpu.roll(twid_ref[:, j * LANES:(j + 1) * LANES], shift, 1)
            outs.append(jnp.where(keep, prev, cur))
            prev = cur
        outs.append(jnp.where(keep, prev, 0.0))
        t_ref[
            pl.ds(pl.multiple_of(b * nq, nq), nq),
            pl.ds(pl.multiple_of(tile * LANES, LANES), NFFT + LANES),
        ] = jnp.concatenate(outs, axis=1).astype(jnp.bfloat16)


def split2(value):
    high = value.astype(jnp.bfloat16)
    low = (value - high.astype(jnp.float32)).astype(jnp.bfloat16)
    return jnp.concatenate([high, low], axis=0)


def main_kernel(dims, t_ref, xr_ref, sq_ref, quad_ref, w_ref, modes_ref, energy_ref,
                qs, ys, sqbuf, zsend, zrecv, zall, sems):
    (length, nvar, ctile, nblock, nbins, nmode, n_x, n_y, per, grid_points) = dims
    n = n_x * n_y
    me = lax.axis_index("sx") * n_y + lax.axis_index("sy")

    def coords(k):
        t = lax.rem(me + k, n)
        return t, (t // n_y, lax.rem(t, n_y))

    barrier = pltpu.get_barrier_semaphore()

    def greet(k, carry):
        _, where = coords(k)
        pl.semaphore_signal(barrier, inc=1, device_id=where, device_id_type=MESH)
        return carry

    lax.fori_loop(1, n, greet, 0)
    pl.semaphore_wait(barrier, n - 1)

    def spread(src, dst, phase, by_target):
        def go(k, carry):
            t, where = coords(k)
            pltpu.make_async_remote_copy(
                src_ref=src.at[t] if by_target else src,
                dst_ref=dst.at[me],
                send_sem=sems.at[2 * phase],
                recv_sem=sems.at[2 * phase + 1],
                device_id=where,
                device_id_type=MESH,
            ).start()
            return carry

        lax.fori_loop(1, n, go, 0)

    def wait_all(dst, sem):
        rest = dst.at[pl.ds(0, n - 1)]
        pltpu.make_async_copy(rest, rest, sems.at[sem]).wait()

    spread(sq_ref, sqbuf, 0, False)

    nq = 2 * nbins
    chunk = nblock * nq // 4
    for j in range(ctile // 2):
        @pl.loop(0, 4)
        def _(i):
            at = pl.ds(pl.multiple_of(i * chunk, chunk), chunk)
            out = jnp.dot(
                t_ref[at, :length],
                xr_ref[:, 2 * j * LANES:2 * (j + 1) * LANES],
                preferred_element_type=jnp.float32,
            )
            qs[2 * j, at, :] = out[:, :LANES]
            qs[2 * j + 1, at, :] = out[:, LANES:]

    wait_all(sqbuf, 1)
    sqbuf[me] = sq_ref[...]
    total = jnp.sum(sqbuf[...], axis=0)
    scale = lax.rsqrt(total / (length * grid_points) + EPS)
    lane = lax.broadcasted_iota(jnp.int32, (1, LANES), 1)
    per_var = ctile // nvar
    cols = []
    for c in range(ctile):
        one = jnp.sum(jnp.where(lane == c // per_var, scale, 0.0), axis=1, keepdims=True)
        cols.append(one * jnp.sqrt(quad_ref[c:c + 1, :]))

    low_half = lax.broadcasted_iota(jnp.int32, (nmode, LANES), 1) < nblock
    pieces = nmode // per if per < nmode else 1
    for f in range(nbins):
        for c in range(ctile):
            for p in range(2):
                part = qs[c, pl.ds(2 * f + p, nblock, stride=nq), :]
                ys[f, p * nblock:(p + 1) * nblock, c * LANES:(c + 1) * LANES] = (
                    part * cols[c]
                ).astype(jnp.bfloat16)
        y = ys[f]
        u = jnp.dot(split2(w_ref[f]), y, preferred_element_type=jnp.float32)
        u = u[:2 * nmode] + u[2 * nmode:]
        a = lax.dot_general(
            split2(u), y, (((1,), (1,)), ((), ())), preferred_element_type=jnp.float32
        )
        a = (a[:2 * nmode] + a[2 * nmode:]) * (1.0 / (3.0 * grid_points))
        up = a[:nmode]
        z = pltpu.roll(a[nmode:], nblock, 1) + jnp.where(low_half, up, -up)
        for s in range(nmode // per):
            zsend[f * (nmode // per) + s] = z[s * per:(s + 1) * per]
    owners = nbins * nmode // per
    for s in range(owners, n):
        zsend[s] = jnp.zeros((per, LANES), jnp.float32)

    spread(zsend, zrecv, 1, True)
    wait_all(zrecv, 3)
    zrecv[me] = zsend[me]
    mine = jnp.sum(zrecv[...], axis=0)
    zall[me] = mine
    spread(zall.at[me], zall, 2, False)
    wait_all(zall, 5)
    wait_all(zrecv, 2)
    wait_all(zall, 4)
    wait_all(sqbuf, 0)

    for f in range(nbins):
        base = f * (nmode // per)
        z = jnp.concatenate([zall[base + s] for s in range(nmode // per)], axis=0)
        norms = jnp.sum(z * z, axis=1, keepdims=True)
        energy_ref[f] = jnp.broadcast_to(jnp.sqrt(norms / nblock), (nmode, LANES))
        coef = z * lax.rsqrt(norms + EPS)
        lhs = jnp.concatenate(
            [jnp.where(low_half, coef, -coef), pltpu.roll(coef, nblock, 1)], axis=0
        ).astype(jnp.bfloat16)
        m = jnp.dot(lhs, ys[f], preferred_element_type=jnp.float32)
        for c in range(ctile):
            modes_ref[pl.ds(f * 2 * nmode * ctile + c, 2 * nmode, stride=ctile), :] = (
                m[:, c * LANES:(c + 1) * LANES]
            )


def shards(n_x, n_y, snapshots, quad_weight, mode_guess, bins, starts):
    length, nvar, cols_x, cols_y = snapshots.shape
    nbins = bins.shape[0]
    nblock = starts.shape[0]
    nmode = mode_guess.shape[-1]
    ctile = nvar * cols_x
    points = ctile * cols_y
    nq = 2 * nbins
    n = n_x * n_y
    grid_points = cols_x * cols_y * n
    vmem = pl.BlockSpec(memory_space=pltpu.VMEM)
    smem = pl.BlockSpec(memory_space=pltpu.SMEM)
    limit = 60 * 1024 * 1024

    twid = make_twiddle(bins).reshape(nq, NFFT).astype(jnp.float32)
    x = snapshots.reshape(length * ctile, cols_y)
    quad = quad_weight.reshape(ctile, cols_y)
    guess_re = jnp.swapaxes(mode_guess[:, :, 0], 1, 2)
    guess_im = jnp.swapaxes(mode_guess[:, :, 1], 1, 2)
    w = jnp.concatenate(
        [
            jnp.concatenate([guess_re, -guess_im], axis=2),
            jnp.concatenate([guess_im, guess_re], axis=2),
        ],
        axis=1,
    )

    t, xr, sq = pl.pallas_call(
        functools.partial(prep_kernel, (length, nvar, ctile, nblock, nq)),
        name="prep",
        out_shape=(
            jax.ShapeDtypeStruct((nblock * nq, length + LANES), jnp.bfloat16),
            jax.ShapeDtypeStruct((length, points), jnp.bfloat16),
            jax.ShapeDtypeStruct((1, LANES), jnp.float32),
        ),
        in_specs=[smem, vmem, vmem, vmem],
        out_specs=(vmem, vmem, vmem),
        scratch_shapes=[pltpu.VMEM((length * ctile, cols_y), jnp.float32)],
        compiler_params=pltpu.CompilerParams(vmem_limit_bytes=limit // 2),
    )(starts, x, quad, twid)

    per = max(1, nbins * nmode // n)
    dims = (length, nvar, ctile, nblock, nbins, nmode, n_x, n_y, per, grid_points)
    modes, energy = pl.pallas_call(
        functools.partial(main_kernel, dims),
        name="spod",
        out_shape=(
            jax.ShapeDtypeStruct((nbins * 2 * nmode * ctile, cols_y), jnp.float32),
            jax.ShapeDtypeStruct((nbins, nmode, LANES), jnp.float32),
        ),
        in_specs=[vmem] * 5,
        out_specs=(vmem, vmem),
        scratch_shapes=[
            pltpu.VMEM((ctile, nblock * nq, LANES), jnp.float32),
            pltpu.VMEM((nbins, 2 * nblock, points), jnp.bfloat16),
            pltpu.VMEM((n, 1, LANES), jnp.float32),
            pltpu.VMEM((n, per, LANES), jnp.float32),
            pltpu.VMEM((n, per, LANES), jnp.float32),
            pltpu.VMEM((n, per, LANES), jnp.float32),
            pltpu.SemaphoreType.DMA((6,)),
        ],
        compiler_params=pltpu.CompilerParams(
            collective_id=0, has_side_effects=True, vmem_limit_bytes=limit // 2
        ),
    )(t, xr, sq, quad, w)
    return (
        modes.reshape(nbins, 2, nmode, nvar, cols_x, cols_y),
        energy[:, :, 0],
    )


def solution(mesh):
    n_x, n_y = mesh.shape["sx"], mesh.shape["sy"]
    return jax.shard_map(
        functools.partial(shards, n_x, n_y),
        mesh=mesh,
        in_specs=(P(None, None, "sx", "sy"), P(None, "sx", "sy"), P(), P(), P()),
        out_specs=(P(None, None, None, None, "sx", "sy"), P()),
        check_vma=False,
    )
```

```python
import functools
import jax
import jax.numpy as jnp
from jax import lax
from jax.experimental import pallas as pl
from jax.experimental.pallas import tpu as pltpu
from jax.sharding import PartitionSpec as P

NFFT = 256
LANES = 128
EPS = 1e-06
MESH = pl.DeviceIdType.MESH


def twiddle_kernel(dims, starts, bins, t_ref, tw):
    nblock, nbins = dims
    nq = 2 * nbins

    shape = (nbins, NFFT)
    row = lax.broadcasted_iota(jnp.int32, shape, 0)
    step = lax.broadcasted_iota(jnp.int32, shape, 1)
    number = jnp.zeros(shape, jnp.int32)
    for f in range(nbins):
        number = jnp.where(row == f, bins[f], number)
    turn = 2.0 * jnp.pi / NFFT
    window = 0.5 - 0.5 * jnp.cos(step.astype(jnp.float32) * turn)
    norm_c = lax.rsqrt(jnp.sum(window * window, axis=1, keepdims=True))
    phase = lax.rem(number * step, NFFT)
    angle = phase.astype(jnp.float32) * turn
    tw[:nbins, :] = norm_c * window * jnp.cos(angle)
    tw[nbins:, :] = -(norm_c * window) * jnp.sin(angle)

    tiles = NFFT // LANES
    wide = lax.broadcasted_iota(jnp.int32, (nq, LANES), 1)
    t_ref[...] = jnp.zeros_like(t_ref)

    def place(b, carry):
        start = starts[b]
        tile = start // LANES
        shift = start - tile * LANES
        keep = wide < shift
        prev = jnp.zeros((nq, LANES), jnp.float32)
        outs = []
        for j in range(tiles):
            cur = pltpu.roll(tw[:, j * LANES:(j + 1) * LANES], shift, 1)
            outs.append(jnp.where(keep, prev, cur))
            prev = cur
        outs.append(jnp.where(keep, prev, 0.0))
        t_ref[
            pl.ds(pl.multiple_of(b * nq, nq), nq),
            pl.ds(pl.multiple_of(tile * LANES, LANES), NFFT + LANES),
        ] = jnp.concatenate(outs, axis=1).astype(jnp.bfloat16)
        return carry

    lax.fori_loop(0, nblock, place, 0, unroll=4)


def split2(value):
    high = value.astype(jnp.bfloat16)
    low = (value - high.astype(jnp.float32)).astype(jnp.bfloat16)
    return jnp.concatenate([high, low], axis=0)


def main_kernel(dims, t_ref, x_ref, quad_ref, guess_ref, y_ref, z_ref,
                xs, xr, sq, qs, sqbuf, zsend, zrecv, zall, sems):
    (length, nvar, ctile, nblock, nbins, nmode, n_x, n_y, per, grid_points) = dims
    n = n_x * n_y
    me = lax.axis_index("sx") * n_y + lax.axis_index("sy")
    per_var = ctile // nvar

    def coords(k):
        t = lax.rem(me + k, n)
        return t, (t // n_y, lax.rem(t, n_y))

    barrier = pltpu.get_barrier_semaphore()

    def greet(k, carry):
        _, where = coords(k)
        pl.semaphore_signal(barrier, inc=1, device_id=where, device_id_type=MESH)
        return carry

    lax.fori_loop(1, n, greet, 0)

    def spread(src, dst, phase, by_target):
        def go(k, carry):
            t, where = coords(k)
            pltpu.make_async_remote_copy(
                src_ref=src.at[t] if by_target else src,
                dst_ref=dst.at[me],
                send_sem=sems.at[2 * phase],
                recv_sem=sems.at[2 * phase + 1],
                device_id=where,
                device_id_type=MESH,
            ).start()
            return carry

        lax.fori_loop(1, n, go, 0)

    def wait_all(dst, sem):
        rest = dst.at[pl.ds(0, n - 1)]
        pltpu.make_async_copy(rest, rest, sems.at[sem]).wait()

    rows = x_ref.shape[0]
    step = rows // 16

    @pl.loop(0, 16)
    def _(i):
        at = pl.ds(pl.multiple_of(i * step, step), step)
        xs[at, :] = x_ref[at, :].astype(jnp.float32)

    lane = lax.broadcasted_iota(jnp.int32, (1, LANES), 1)
    quads = [quad_ref[c // per_var, c % per_var:c % per_var + 1, :] for c in range(ctile)]
    total = jnp.zeros((1, LANES), jnp.float32)
    for c in range(ctile):
        col = xs[pl.ds(c, length, stride=ctile), :]
        xr[:, c * LANES:(c + 1) * LANES] = col.astype(jnp.bfloat16)
        sums = jnp.sum(col * col, axis=0, keepdims=True) * quads[c]
        one = jnp.sum(sums, axis=1, keepdims=True)
        total = total + jnp.where(lane == c // per_var, one, 0.0)
    sq[...] = total

    pl.semaphore_wait(barrier, n - 1)
    spread(sq, sqbuf, 0, False)

    nq = 2 * nbins
    chunk = nblock * nq // 4
    for j in range(ctile // 2):
        @pl.loop(0, 4)
        def _(i):
            at = pl.ds(pl.multiple_of(i * chunk, chunk), chunk)
            out = jnp.dot(
                t_ref[at, :length],
                xr[:, 2 * j * LANES:2 * (j + 1) * LANES],
                preferred_element_type=jnp.float32,
            )
            qs[2 * j, at, :] = out[:, :LANES]
            qs[2 * j + 1, at, :] = out[:, LANES:]

    wait_all(sqbuf, 1)
    sqbuf[me] = sq[...]
    total = jnp.sum(sqbuf[...], axis=0)
    scale = lax.rsqrt(total / (length * grid_points) + EPS)
    cols = []
    for c in range(ctile):
        one = jnp.sum(jnp.where(lane == c // per_var, scale, 0.0), axis=1, keepdims=True)
        cols.append(one * jnp.sqrt(quads[c]))

    low_half = lax.broadcasted_iota(jnp.int32, (nmode, LANES), 1) < nblock
    parts = nmode // per
    for f in range(nbins):
        for c in range(ctile):
            for p in range(2):
                part = qs[c, pl.ds(p * nbins + f, nblock, stride=nq), :]
                y_ref[f, p * nblock:(p + 1) * nblock, c * LANES:(c + 1) * LANES] = (
                    part * cols[c]
                ).astype(jnp.bfloat16)
        y = y_ref[f]
        g_re, g_im = guess_ref[f, 0], guess_ref[f, 1]
        w = jnp.concatenate(
            [
                jnp.concatenate([g_re, -g_im], axis=1),
                jnp.concatenate([g_im, g_re], axis=1),
            ],
            axis=0,
        )
        u = jnp.dot(split2(w), y, preferred_element_type=jnp.float32)
        u = u[:2 * nmode] + u[2 * nmode:]
        a = lax.dot_general(
            split2(u), y, (((1,), (1,)), ((), ())), preferred_element_type=jnp.float32
        )
        a = (a[:2 * nmode] + a[2 * nmode:]) * (1.0 / (3.0 * grid_points))
        up = a[:nmode]
        z = pltpu.roll(a[nmode:], nblock, 1) + jnp.where(low_half, up, -up)
        for s in range(parts):
            zsend[f * parts + s] = z[s * per:(s + 1) * per]
    owners = nbins * parts
    for s in range(owners, n):
        zsend[s] = jnp.zeros((per, LANES), jnp.float32)

    spread(zsend, zrecv, 1, True)
    wait_all(zrecv, 3)
    zrecv[me] = zsend[me]
    zall[me] = jnp.sum(zrecv[...], axis=0)
    spread(zall.at[me], zall, 2, False)
    wait_all(zall, 5)
    for s in range(owners):
        z_ref[s * per:(s + 1) * per] = zall[s]
    wait_all(zrecv, 2)
    wait_all(zall, 4)
    wait_all(sqbuf, 0)


def modes_kernel(dims, y_ref, z_ref, modes_hbm, energy_ref, out, sems):
    ctile, nblock, nbins, nmode = dims
    span = 2 * nmode * ctile
    low_half = lax.broadcasted_iota(jnp.int32, (nmode, LANES), 1) < nblock
    column = lax.broadcasted_iota(jnp.int32, (nmode, nbins), 1)
    energy = jnp.zeros((nmode, nbins), jnp.float32)

    def store(f):
        at = pl.ds(f * span, span)
        return pltpu.make_async_copy(out.at[at], modes_hbm.at[at], sems.at[f])

    for f in range(nbins):
        z = z_ref[f * nmode:(f + 1) * nmode]
        norms = jnp.sum(z * z, axis=1, keepdims=True)
        energy = jnp.where(column == f, jnp.sqrt(norms / nblock), energy)
        coef = z * lax.rsqrt(norms + EPS)
        lhs = jnp.concatenate(
            [jnp.where(low_half, coef, -coef), pltpu.roll(coef, nblock, 1)], axis=0
        ).astype(jnp.bfloat16)
        m = jnp.dot(lhs, y_ref[f], preferred_element_type=jnp.float32)
        for c in range(ctile):
            out[pl.ds(f * span + c, 2 * nmode, stride=ctile), :] = (
                m[:, c * LANES:(c + 1) * LANES]
            )
        if f > 0:
            store(f - 1).start()
    energy_ref[...] = energy
    store(nbins - 1).start()
    for f in range(nbins):
        store(f).wait()


def shards(n_x, n_y, snapshots, quad_weight, mode_guess, bins, starts):
    length, nvar, cols_x, cols_y = snapshots.shape
    nbins = bins.shape[0]
    nblock = starts.shape[0]
    nmode = mode_guess.shape[-1]
    ctile = nvar * cols_x
    points = ctile * cols_y
    nq = 2 * nbins
    n = n_x * n_y
    grid_points = cols_x * cols_y * n
    vmem = pl.BlockSpec(memory_space=pltpu.VMEM)
    smem = pl.BlockSpec(memory_space=pltpu.SMEM)
    hbm = pl.BlockSpec(memory_space=pltpu.HBM)
    limit = 30 * 1024 * 1024

    x = snapshots.reshape(length * ctile, cols_y)
    guess = jnp.transpose(mode_guess, (0, 2, 3, 1))

    t = pl.pallas_call(
        functools.partial(twiddle_kernel, (nblock, nbins)),
        name="twiddle",
        out_shape=jax.ShapeDtypeStruct((nblock * nq, length + LANES), jnp.bfloat16),
        in_specs=[smem, smem],
        out_specs=vmem,
        scratch_shapes=[pltpu.VMEM((nq, NFFT), jnp.float32)],
        compiler_params=pltpu.CompilerParams(vmem_limit_bytes=limit),
        cost_estimate=pl.CostEstimate(
            flops=0, transcendentals=0, bytes_accessed=2 * nblock * nq * (length + LANES)
        ),
    )(starts, bins)

    per = max(1, nbins * nmode // n)
    dims = (length, nvar, ctile, nblock, nbins, nmode, n_x, n_y, per, grid_points)
    y, z = pl.pallas_call(
        functools.partial(main_kernel, dims),
        name="spod",
        out_shape=(
            jax.ShapeDtypeStruct((nbins, 2 * nblock, points), jnp.bfloat16),
            jax.ShapeDtypeStruct((nbins * nmode, LANES), jnp.float32),
        ),
        in_specs=[vmem] * 4,
        out_specs=(vmem, vmem),
        scratch_shapes=[
            pltpu.VMEM((length * ctile, cols_y), jnp.float32),
            pltpu.VMEM((length, points), jnp.bfloat16),
            pltpu.VMEM((1, LANES), jnp.float32),
            pltpu.VMEM((ctile, nblock * nq, LANES), jnp.float32),
            pltpu.VMEM((n, 1, LANES), jnp.float32),
            pltpu.VMEM((n, per, LANES), jnp.float32),
            pltpu.VMEM((n, per, LANES), jnp.float32),
            pltpu.VMEM((n, per, LANES), jnp.float32),
            pltpu.SemaphoreType.DMA((6,)),
        ],
        compiler_params=pltpu.CompilerParams(
            collective_id=0, has_side_effects=True, vmem_limit_bytes=limit
        ),
    )(t, x, quad_weight, guess)

    modes, energy = pl.pallas_call(
        functools.partial(modes_kernel, (ctile, nblock, nbins, nmode)),
        name="modes",
        out_shape=(
            jax.ShapeDtypeStruct((nbins * 2 * nmode * ctile, cols_y), jnp.float32),
            jax.ShapeDtypeStruct((nmode, nbins), jnp.float32),
        ),
        in_specs=[vmem, vmem],
        out_specs=(hbm, vmem),
        scratch_shapes=[
            pltpu.VMEM((nbins * 2 * nmode * ctile, cols_y), jnp.float32),
            pltpu.SemaphoreType.DMA((nbins,)),
        ],
        compiler_params=pltpu.CompilerParams(vmem_limit_bytes=limit),
    )(y, z)
    return (
        modes.reshape(nbins, 2, nmode, nvar, cols_x, cols_y),
        energy.T,
    )


def solution(mesh):
    n_x, n_y = mesh.shape["sx"], mesh.shape["sy"]
    return jax.shard_map(
        functools.partial(shards, n_x, n_y),
        mesh=mesh,
        in_specs=(P(None, None, "sx", "sy"), P(None, "sx", "sy"), P(), P(), P()),
        out_specs=(P(None, None, None, None, "sx", "sy"), P()),
        check_vma=False,
    )
```

```python
import functools
import jax
import jax.numpy as jnp
from jax import lax
from jax.experimental import pallas as pl
from jax.experimental.pallas import tpu as pltpu
from jax.sharding import PartitionSpec as P

NFFT = 256
LANES = 128
EPS = 1e-06
MESH = pl.DeviceIdType.MESH


def fill_twiddle(bins, nbins, tw):
    shape = (nbins, NFFT)
    row = lax.broadcasted_iota(jnp.int32, shape, 0)
    step = lax.broadcasted_iota(jnp.int32, shape, 1)
    number = jnp.zeros(shape, jnp.int32)
    for f in range(nbins):
        number = jnp.where(row == f, bins[f], number)
    turn = 2.0 * jnp.pi / NFFT
    window = 0.5 - 0.5 * jnp.cos(step.astype(jnp.float32) * turn)
    norm_c = lax.rsqrt(jnp.sum(window * window, axis=1, keepdims=True))
    phase = lax.rem(number * step, NFFT)
    angle = phase.astype(jnp.float32) * turn
    tw[:nbins, :] = norm_c * window * jnp.cos(angle)
    tw[nbins:, :] = -(norm_c * window) * jnp.sin(angle)


def shifted_rows(start, nq, length, tw):
    tile = start // LANES
    shift = start - tile * LANES
    wide = lax.broadcasted_iota(jnp.int32, (nq, LANES), 1)
    keep = wide < shift
    zero = jnp.zeros((nq, LANES), jnp.float32)
    prev, pieces = zero, []
    for j in range(NFFT // LANES):
        cur = pltpu.roll(tw[:, j * LANES:(j + 1) * LANES], shift, 1)
        pieces.append(jnp.where(keep, prev, cur))
        prev = cur
    pieces.append(jnp.where(keep, prev, zero))
    outs = []
    for j in range(length // LANES):
        out = zero
        for i, piece in enumerate(pieces):
            out = jnp.where(tile + i == j, piece, out)
        outs.append(out)
    return jnp.concatenate(outs, axis=1).astype(jnp.bfloat16)


def split2(value):
    high = value.astype(jnp.bfloat16)
    low = (value - high.astype(jnp.float32)).astype(jnp.bfloat16)
    return jnp.concatenate([high, low], axis=0)


def main_kernel(dims, starts_hbm, bins_hbm, x_hbm, quad_hbm, guess_hbm, y_ref, z_ref,
                starts, bins, x_ref, quad_ref, guess_ref, t_ref, tw, xs, xr, sq, qs,
                sqbuf, zsend, zrecv, zall, load_sems, sems):
    (length, nvar, ctile, nblock, nbins, nmode, n_x, n_y, per, grid_points) = dims
    n = n_x * n_y
    me = lax.axis_index("sx") * n_y + lax.axis_index("sy")
    per_var = ctile // nvar
    nq = 2 * nbins
    loads = [
        pltpu.make_async_copy(src, dst, load_sems.at[i])
        for i, (src, dst) in enumerate(
            [
                (bins_hbm, bins),
                (starts_hbm, starts),
                (quad_hbm, quad_ref),
                (x_hbm, x_ref),
                (guess_hbm, guess_ref),
            ]
        )
    ]
    for load in loads:
        load.start()

    def coords(k):
        t = lax.rem(me + k, n)
        return t, (t // n_y, lax.rem(t, n_y))

    barrier = pltpu.get_barrier_semaphore()

    def greet(k, carry):
        _, where = coords(k)
        pl.semaphore_signal(barrier, inc=1, device_id=where, device_id_type=MESH)
        return carry

    lax.fori_loop(1, n, greet, 0)

    def spread(src, dst, phase, by_target):
        def go(k, carry):
            t, where = coords(k)
            pltpu.make_async_remote_copy(
                src_ref=src.at[t] if by_target else src,
                dst_ref=dst.at[me],
                send_sem=sems.at[2 * phase],
                recv_sem=sems.at[2 * phase + 1],
                device_id=where,
                device_id_type=MESH,
            ).start()
            return carry

        lax.fori_loop(1, n, go, 0)

    def wait_all(dst, sem):
        rest = dst.at[pl.ds(0, n - 1)]
        pltpu.make_async_copy(rest, rest, sems.at[sem]).wait()

    loads[0].wait()
    fill_twiddle(bins, nbins, tw)
    for load in loads[1:]:
        load.wait()
    rows = x_ref.shape[0]
    step = rows // 16

    @pl.loop(0, 16)
    def _(i):
        at = pl.ds(pl.multiple_of(i * step, step), step)
        xs[at, :] = x_ref[at, :].astype(jnp.float32)

    lane = lax.broadcasted_iota(jnp.int32, (1, LANES), 1)
    quads = [quad_ref[c // per_var, c % per_var:c % per_var + 1, :] for c in range(ctile)]
    total = jnp.zeros((1, LANES), jnp.float32)
    for c in range(ctile):
        col = xs[pl.ds(c, length, stride=ctile), :]
        xr[:, c * LANES:(c + 1) * LANES] = col.astype(jnp.bfloat16)
        sums = jnp.sum(col * col, axis=0, keepdims=True) * quads[c]
        one = jnp.sum(sums, axis=1, keepdims=True)
        total = total + jnp.where(lane == c // per_var, one, 0.0)
    sq[...] = total

    pl.semaphore_wait(barrier, n - 1)
    spread(sq, sqbuf, 0, False)

    @pl.loop(0, nblock // 4)
    def _(i):
        for k in range(4):
            b = i * 4 + k
            t_ref[pl.ds(pl.multiple_of(b * nq, nq), nq), :] = shifted_rows(
                starts[b], nq, length, tw
            )

    chunk = nblock * nq // 4
    for j in range(ctile // 2):
        @pl.loop(0, 4)
        def _(i):
            at = pl.ds(pl.multiple_of(i * chunk, chunk), chunk)
            out = jnp.dot(
                t_ref[at, :],
                xr[:, 2 * j * LANES:2 * (j + 1) * LANES],
                preferred_element_type=jnp.float32,
            )
            qs[2 * j, at, :] = out[:, :LANES]
            qs[2 * j + 1, at, :] = out[:, LANES:]

    wait_all(sqbuf, 1)
    sqbuf[me] = sq[...]
    total = jnp.sum(sqbuf[...], axis=0)
    scale = lax.rsqrt(total / (length * grid_points) + EPS)
    cols = []
    for c in range(ctile):
        one = jnp.sum(jnp.where(lane == c // per_var, scale, 0.0), axis=1, keepdims=True)
        cols.append(one * jnp.sqrt(quads[c]))

    low_half = lax.broadcasted_iota(jnp.int32, (nmode, LANES), 1) < nblock
    parts = nmode // per
    for f in range(nbins):
        for c in range(ctile):
            for p in range(2):
                part = qs[c, pl.ds(p * nbins + f, nblock, stride=nq), :]
                y_ref[f, p * nblock:(p + 1) * nblock, c * LANES:(c + 1) * LANES] = (
                    part * cols[c]
                ).astype(jnp.bfloat16)
        y = y_ref[f]
        g_re, g_im = guess_ref[f, 0], guess_ref[f, 1]
        w = jnp.concatenate(
            [
                jnp.concatenate([g_re, -g_im], axis=1),
                jnp.concatenate([g_im, g_re], axis=1),
            ],
            axis=0,
        )
        u = jnp.dot(split2(w), y, preferred_element_type=jnp.float32)
        u = u[:2 * nmode] + u[2 * nmode:]
        a = lax.dot_general(
            split2(u), y, (((1,), (1,)), ((), ())), preferred_element_type=jnp.float32
        )
        a = (a[:2 * nmode] + a[2 * nmode:]) * (1.0 / (3.0 * grid_points))
        up = a[:nmode]
        z = pltpu.roll(a[nmode:], nblock, 1) + jnp.where(low_half, up, -up)
        for s in range(parts):
            zsend[f * parts + s] = z[s * per:(s + 1) * per]
    owners = nbins * parts
    for s in range(owners, n):
        zsend[s] = jnp.zeros((per, LANES), jnp.float32)

    spread(zsend, zrecv, 1, True)
    wait_all(zrecv, 3)
    zrecv[me] = zsend[me]
    zall[me] = jnp.sum(zrecv[...], axis=0)
    spread(zall.at[me], zall, 2, False)
    wait_all(zall, 5)
    for s in range(owners):
        z_ref[s * per:(s + 1) * per] = zall[s]
    wait_all(zrecv, 2)
    wait_all(zall, 4)
    wait_all(sqbuf, 0)


def modes_kernel(dims, y_ref, z_ref, modes_hbm, energy_ref, out, sems):
    ctile, nblock, nbins, nmode = dims
    span = 2 * nmode * ctile
    low_half = lax.broadcasted_iota(jnp.int32, (nmode, LANES), 1) < nblock
    column = lax.broadcasted_iota(jnp.int32, (nmode, nbins), 1)
    energy = jnp.zeros((nmode, nbins), jnp.float32)

    def store(f):
        at = pl.ds(f * span, span)
        return pltpu.make_async_copy(out.at[at], modes_hbm.at[at], sems.at[f])

    for f in range(nbins):
        z = z_ref[f * nmode:(f + 1) * nmode]
        norms = jnp.sum(z * z, axis=1, keepdims=True)
        energy = jnp.where(column == f, jnp.sqrt(norms / nblock), energy)
        coef = z * lax.rsqrt(norms + EPS)
        lhs = jnp.concatenate(
            [jnp.where(low_half, coef, -coef), pltpu.roll(coef, nblock, 1)], axis=0
        ).astype(jnp.bfloat16)
        m = jnp.dot(lhs, y_ref[f], preferred_element_type=jnp.float32)
        for c in range(ctile):
            out[pl.ds(f * span + c, 2 * nmode, stride=ctile), :] = (
                m[:, c * LANES:(c + 1) * LANES]
            )
        if f > 0:
            store(f - 1).start()
    energy_ref[...] = energy
    store(nbins - 1).start()
    for f in range(nbins):
        store(f).wait()


def shards(n_x, n_y, snapshots, quad_weight, mode_guess, bins, starts):
    length, nvar, cols_x, cols_y = snapshots.shape
    nbins = bins.shape[0]
    nblock = starts.shape[0]
    nmode = mode_guess.shape[-1]
    ctile = nvar * cols_x
    points = ctile * cols_y
    nq = 2 * nbins
    n = n_x * n_y
    grid_points = cols_x * cols_y * n
    vmem = pl.BlockSpec(memory_space=pltpu.VMEM)
    hbm = pl.BlockSpec(memory_space=pltpu.HBM)
    limit = 30 * 1024 * 1024

    x = snapshots.reshape(length * ctile, cols_y)
    guess = jnp.transpose(mode_guess, (0, 2, 3, 1))

    operands = [
        pltpu.with_memory_space_constraint(value, pltpu.HBM)
        for value in (starts, bins, x, quad_weight, guess)
    ]
    per = max(1, nbins * nmode // n)
    dims = (length, nvar, ctile, nblock, nbins, nmode, n_x, n_y, per, grid_points)
    y, z = pl.pallas_call(
        functools.partial(main_kernel, dims),
        name="spod",
        out_shape=(
            jax.ShapeDtypeStruct((nbins, 2 * nblock, points), jnp.bfloat16),
            jax.ShapeDtypeStruct((nbins * nmode, LANES), jnp.float32),
        ),
        in_specs=[hbm] * 5,
        out_specs=(vmem, vmem),
        scratch_shapes=[
            pltpu.SMEM(starts.shape, jnp.int32),
            pltpu.SMEM(bins.shape, jnp.int32),
            pltpu.VMEM(x.shape, jnp.bfloat16),
            pltpu.VMEM(quad_weight.shape, jnp.float32),
            pltpu.VMEM(guess.shape, jnp.float32),
            pltpu.VMEM((nblock * nq, length), jnp.bfloat16),
            pltpu.VMEM((nq, NFFT), jnp.float32),
            pltpu.VMEM((length * ctile, cols_y), jnp.float32),
            pltpu.VMEM((length, points), jnp.bfloat16),
            pltpu.VMEM((1, LANES), jnp.float32),
            pltpu.VMEM((ctile, nblock * nq, LANES), jnp.float32),
            pltpu.VMEM((n, 1, LANES), jnp.float32),
            pltpu.VMEM((n, per, LANES), jnp.float32),
            pltpu.VMEM((n, per, LANES), jnp.float32),
            pltpu.VMEM((n, per, LANES), jnp.float32),
            pltpu.SemaphoreType.DMA((5,)),
            pltpu.SemaphoreType.DMA((6,)),
        ],
        compiler_params=pltpu.CompilerParams(
            collective_id=0, has_side_effects=True, vmem_limit_bytes=limit
        ),
    )(*operands)

    modes, energy = pl.pallas_call(
        functools.partial(modes_kernel, (ctile, nblock, nbins, nmode)),
        name="modes",
        out_shape=(
            jax.ShapeDtypeStruct((nbins * 2 * nmode * ctile, cols_y), jnp.float32),
            jax.ShapeDtypeStruct((nmode, nbins), jnp.float32),
        ),
        in_specs=[vmem, vmem],
        out_specs=(hbm, vmem),
        scratch_shapes=[
            pltpu.VMEM((nbins * 2 * nmode * ctile, cols_y), jnp.float32),
            pltpu.SemaphoreType.DMA((nbins,)),
        ],
        compiler_params=pltpu.CompilerParams(vmem_limit_bytes=limit),
    )(y, z)
    return (
        modes.reshape(nbins, 2, nmode, nvar, cols_x, cols_y),
        energy.T,
    )


def solution(mesh):
    n_x, n_y = mesh.shape["sx"], mesh.shape["sy"]
    return jax.shard_map(
        functools.partial(shards, n_x, n_y),
        mesh=mesh,
        in_specs=(P(None, None, "sx", "sy"), P(None, "sx", "sy"), P(), P(), P()),
        out_specs=(P(None, None, None, None, "sx", "sy"), P()),
        check_vma=False,
    )
```

```python
import functools
import jax
import jax.numpy as jnp
from jax import lax
from jax.experimental import pallas as pl
from jax.experimental.pallas import tpu as pltpu
from jax.sharding import PartitionSpec as P

NFFT = 256
LANES = 128
EPS = 1e-06
MESH = pl.DeviceIdType.MESH


def fill_twiddle(bins, nbins, tw):
    shape = (nbins, NFFT)
    row = lax.broadcasted_iota(jnp.int32, shape, 0)
    step = lax.broadcasted_iota(jnp.int32, shape, 1)
    number = jnp.zeros(shape, jnp.int32)
    for f in range(nbins):
        number = jnp.where(row == f, bins[f], number)
    turn = 2.0 * jnp.pi / NFFT
    window = 0.5 - 0.5 * jnp.cos(step.astype(jnp.float32) * turn)
    norm_c = lax.rsqrt(jnp.sum(window * window, axis=1, keepdims=True))
    phase = lax.rem(number * step, NFFT)
    angle = phase.astype(jnp.float32) * turn
    tw[:nbins, :] = norm_c * window * jnp.cos(angle)
    tw[nbins:, :] = -(norm_c * window) * jnp.sin(angle)


def shifted_rows(start, nq, length, tw):
    tile = start // LANES
    shift = start - tile * LANES
    wide = lax.broadcasted_iota(jnp.int32, (nq, LANES), 1)
    keep = wide < shift
    zero = jnp.zeros((nq, LANES), jnp.float32)
    prev, pieces = zero, []
    for j in range(NFFT // LANES):
        cur = pltpu.roll(tw[:, j * LANES:(j + 1) * LANES], shift, 1)
        pieces.append(jnp.where(keep, prev, cur))
        prev = cur
    pieces.append(jnp.where(keep, prev, zero))
    outs = []
    for j in range(length // LANES):
        out = zero
        for i, piece in enumerate(pieces):
            out = jnp.where(tile + i == j, piece, out)
        outs.append(out)
    return jnp.concatenate(outs, axis=1).astype(jnp.bfloat16)


def split2(value):
    high = value.astype(jnp.bfloat16)
    low = (value - high.astype(jnp.float32)).astype(jnp.bfloat16)
    return jnp.concatenate([high, low], axis=0)


def main_kernel(dims, starts_hbm, bins_hbm, x_hbm, quad_hbm, guess_hbm, y_ref, z_ref,
                starts, bins, x_ref, quad_ref, guess_ref, t_ref, tw, xs, xr, sq, qs,
                w_ref, acc, sqbuf, zsend, zrecv, zall, load_sems, sems):
    (length, nvar, ctile, nblock, nbins, nmode, n_x, n_y, per, grid_points) = dims
    n = n_x * n_y
    me = lax.axis_index("sx") * n_y + lax.axis_index("sy")
    per_var = ctile // nvar
    nq = 2 * nbins
    loads = [
        pltpu.make_async_copy(src, dst, load_sems.at[i])
        for i, (src, dst) in enumerate(
            [
                (bins_hbm, bins),
                (starts_hbm, starts),
                (quad_hbm, quad_ref),
                (x_hbm, x_ref),
                (guess_hbm, guess_ref),
            ]
        )
    ]
    for load in loads:
        load.start()

    ix, iy = lax.axis_index("sx"), lax.axis_index("sy")

    def each_partner(act):
        def pick(dx, dy):
            tx, ty = lax.rem(ix + dx, n_x), lax.rem(iy + dy, n_y)
            act(tx * n_y + ty, (tx, ty))

        for dy in range(1, n_y):
            pick(0, dy)

        def go(dx, carry):
            for dy in range(n_y):
                pick(dx, dy)
            return carry

        lax.fori_loop(1, n_x, go, 0, unroll=5)

    barrier = pltpu.get_barrier_semaphore()
    each_partner(
        lambda t, where: pl.semaphore_signal(
            barrier, inc=1, device_id=where, device_id_type=MESH
        )
    )

    def spread(src, dst, phase, by_target):
        each_partner(
            lambda t, where: pltpu.make_async_remote_copy(
                src_ref=src.at[t] if by_target else src,
                dst_ref=dst.at[me],
                send_sem=sems.at[2 * phase],
                recv_sem=sems.at[2 * phase + 1],
                device_id=where,
                device_id_type=MESH,
            ).start()
        )

    def wait_all(dst, sem):
        rest = dst.at[pl.ds(0, n - 1)]
        pltpu.make_async_copy(rest, rest, sems.at[sem]).wait()

    loads[0].wait()
    fill_twiddle(bins, nbins, tw)
    for load in loads[1:]:
        load.wait()
    rows = x_ref.shape[0]
    step = rows // 16

    @pl.loop(0, 16)
    def _(i):
        at = pl.ds(pl.multiple_of(i * step, step), step)
        xs[at, :] = x_ref[at, :].astype(jnp.float32)

    lane = lax.broadcasted_iota(jnp.int32, (1, LANES), 1)
    quads = [quad_ref[c // per_var, c % per_var:c % per_var + 1, :] for c in range(ctile)]
    total = jnp.zeros((1, LANES), jnp.float32)
    for c in range(ctile):
        col = xs[pl.ds(c, length, stride=ctile), :]
        xr[:, c * LANES:(c + 1) * LANES] = col.astype(jnp.bfloat16)
        sums = jnp.sum(col * col, axis=0, keepdims=True) * quads[c]
        one = jnp.sum(sums, axis=1, keepdims=True)
        total = total + jnp.where(lane == c // per_var, one, 0.0)
    sq[...] = total

    for f in range(nbins):
        g_re, g_im = guess_ref[f, 0], guess_ref[f, 1]
        w_ref[f] = split2(
            jnp.concatenate(
                [
                    jnp.concatenate([g_re, -g_im], axis=1),
                    jnp.concatenate([g_im, g_re], axis=1),
                ],
                axis=0,
            )
        )

    pl.semaphore_wait(barrier, n - 1)
    spread(sq, sqbuf, 0, False)

    @pl.loop(0, nblock // 4)
    def _(i):
        for k in range(4):
            b = i * 4 + k
            t_ref[pl.ds(pl.multiple_of(b * nq, nq), nq), :] = shifted_rows(
                starts[b], nq, length, tw
            )

    chunks = 4
    chunk = nblock * nq // chunks

    def transform(i, j):
        at = slice(i * chunk, (i + 1) * chunk)
        out = jnp.dot(
            t_ref[at, :],
            xr[:, 2 * j * LANES:2 * (j + 1) * LANES],
            preferred_element_type=jnp.float32,
        )
        qs[2 * j, at, :] = out[:, :LANES]
        qs[2 * j + 1, at, :] = out[:, LANES:]

    def fold(value):
        return value[:2 * nmode] + value[2 * nmode:]

    def project(f, j, cols):
        for c in (2 * j, 2 * j + 1):
            for p in range(2):
                part = qs[c, pl.ds(p * nbins + f, nblock, stride=nq), :]
                y_ref[f, p * nblock:(p + 1) * nblock, c * LANES:(c + 1) * LANES] = (
                    part * cols[c]
                ).astype(jnp.bfloat16)
        y = y_ref[f, :, 2 * j * LANES:2 * (j + 1) * LANES]
        u = fold(jnp.dot(w_ref[f], y, preferred_element_type=jnp.float32))
        return fold(
            lax.dot_general(
                split2(u), y, (((1,), (1,)), ((), ())), preferred_element_type=jnp.float32
            )
        )

    pairs = ctile // 2
    share = nbins // chunks
    for i in range(chunks):
        transform(i, 0)

    wait_all(sqbuf, 1)
    sqbuf[me] = sq[...]
    total = jnp.sum(sqbuf[...], axis=0)
    scale = lax.rsqrt(total / (length * grid_points) + EPS)
    cols = []
    for c in range(ctile):
        one = jnp.sum(jnp.where(lane == c // per_var, scale, 0.0), axis=1, keepdims=True)
        cols.append(one * jnp.sqrt(quads[c]))

    for j in range(1, pairs):
        for i in range(chunks):
            transform(i, j)
            for f in range(i * share, (i + 1) * share):
                a = project(f, j - 1, cols)
                acc[f] = a if j == 1 else acc[f] + a

    low_half = lax.broadcasted_iota(jnp.int32, (nmode, LANES), 1) < nblock
    parts = nmode // per
    for f in range(nbins):
        a = project(f, pairs - 1, cols)
        if pairs > 1:
            a = a + acc[f]
        a = a * (1.0 / (3.0 * grid_points))
        up = a[:nmode]
        z = pltpu.roll(a[nmode:], nblock, 1) + jnp.where(low_half, up, -up)
        for s in range(parts):
            zsend[f * parts + s] = z[s * per:(s + 1) * per]
    owners = nbins * parts
    for s in range(owners, n):
        zsend[s] = jnp.zeros((per, LANES), jnp.float32)

    spread(zsend, zrecv, 1, True)
    wait_all(zrecv, 3)
    zrecv[me] = zsend[me]
    zall[me] = jnp.sum(zrecv[...], axis=0)
    spread(zall.at[me], zall, 2, False)
    wait_all(zall, 5)
    for s in range(owners):
        z_ref[s * per:(s + 1) * per] = zall[s]
    wait_all(zrecv, 2)
    wait_all(zall, 4)
    wait_all(sqbuf, 0)


def modes_kernel(dims, y_ref, z_ref, modes_hbm, energy_ref, out, sems):
    ctile, nblock, nbins, nmode = dims
    span = 2 * nmode * ctile
    low_half = lax.broadcasted_iota(jnp.int32, (nmode, LANES), 1) < nblock
    column = lax.broadcasted_iota(jnp.int32, (nmode, nbins), 1)
    energy = jnp.zeros((nmode, nbins), jnp.float32)

    def store(f):
        at = pl.ds(f * span, span)
        return pltpu.make_async_copy(out.at[at], modes_hbm.at[at], sems.at[f])

    for f in range(nbins):
        z = z_ref[f * nmode:(f + 1) * nmode]
        norms = jnp.sum(z * z, axis=1, keepdims=True)
        energy = jnp.where(column == f, jnp.sqrt(norms / nblock), energy)
        coef = z * lax.rsqrt(norms + EPS)
        lhs = jnp.concatenate(
            [jnp.where(low_half, coef, -coef), pltpu.roll(coef, nblock, 1)], axis=0
        ).astype(jnp.bfloat16)
        m = jnp.dot(lhs, y_ref[f], preferred_element_type=jnp.float32)
        for c in range(ctile):
            out[pl.ds(f * span + c, 2 * nmode, stride=ctile), :] = (
                m[:, c * LANES:(c + 1) * LANES]
            )
        if f > 0:
            store(f - 1).start()
    energy_ref[...] = energy
    store(nbins - 1).start()
    for f in range(nbins):
        store(f).wait()


def shards(n_x, n_y, snapshots, quad_weight, mode_guess, bins, starts):
    length, nvar, cols_x, cols_y = snapshots.shape
    nbins = bins.shape[0]
    nblock = starts.shape[0]
    nmode = mode_guess.shape[-1]
    ctile = nvar * cols_x
    points = ctile * cols_y
    nq = 2 * nbins
    n = n_x * n_y
    grid_points = cols_x * cols_y * n
    vmem = pl.BlockSpec(memory_space=pltpu.VMEM)
    hbm = pl.BlockSpec(memory_space=pltpu.HBM)
    limit = 30 * 1024 * 1024

    x = snapshots.reshape(length * ctile, cols_y)
    guess = jnp.transpose(mode_guess, (0, 2, 3, 1))

    operands = [
        pltpu.with_memory_space_constraint(value, pltpu.HBM)
        for value in (starts, bins, x, quad_weight, guess)
    ]
    per = max(1, nbins * nmode // n)
    dims = (length, nvar, ctile, nblock, nbins, nmode, n_x, n_y, per, grid_points)
    y, z = pl.pallas_call(
        functools.partial(main_kernel, dims),
        name="spod",
        out_shape=(
            jax.ShapeDtypeStruct((nbins, 2 * nblock, points), jnp.bfloat16),
            jax.ShapeDtypeStruct((nbins * nmode, LANES), jnp.float32),
        ),
        in_specs=[hbm] * 5,
        out_specs=(vmem, vmem),
        scratch_shapes=[
            pltpu.SMEM(starts.shape, jnp.int32),
            pltpu.SMEM(bins.shape, jnp.int32),
            pltpu.VMEM(x.shape, jnp.bfloat16),
            pltpu.VMEM(quad_weight.shape, jnp.float32),
            pltpu.VMEM(guess.shape, jnp.float32),
            pltpu.VMEM((nblock * nq, length), jnp.bfloat16),
            pltpu.VMEM((nq, NFFT), jnp.float32),
            pltpu.VMEM((length * ctile, cols_y), jnp.float32),
            pltpu.VMEM((length, points), jnp.bfloat16),
            pltpu.VMEM((1, LANES), jnp.float32),
            pltpu.VMEM((ctile, nblock * nq, LANES), jnp.float32),
            pltpu.VMEM((nbins, 4 * nmode, 2 * nblock), jnp.bfloat16),
            pltpu.VMEM((nbins, 2 * nmode, LANES), jnp.float32),
            pltpu.VMEM((n, 1, LANES), jnp.float32),
            pltpu.VMEM((n, per, LANES), jnp.float32),
            pltpu.VMEM((n, per, LANES), jnp.float32),
            pltpu.VMEM((n, per, LANES), jnp.float32),
            pltpu.SemaphoreType.DMA((5,)),
            pltpu.SemaphoreType.DMA((6,)),
        ],
        compiler_params=pltpu.CompilerParams(
            collective_id=0, has_side_effects=True, vmem_limit_bytes=limit
        ),
    )(*operands)

    modes, energy = pl.pallas_call(
        functools.partial(modes_kernel, (ctile, nblock, nbins, nmode)),
        name="modes",
        out_shape=(
            jax.ShapeDtypeStruct((nbins * 2 * nmode * ctile, cols_y), jnp.float32),
            jax.ShapeDtypeStruct((nmode, nbins), jnp.float32),
        ),
        in_specs=[vmem, vmem],
        out_specs=(hbm, vmem),
        scratch_shapes=[
            pltpu.VMEM((nbins * 2 * nmode * ctile, cols_y), jnp.float32),
            pltpu.SemaphoreType.DMA((nbins,)),
        ],
        compiler_params=pltpu.CompilerParams(vmem_limit_bytes=limit),
    )(y, z)
    return (
        modes.reshape(nbins, 2, nmode, nvar, cols_x, cols_y),
        energy.T,
    )


def solution(mesh):
    n_x, n_y = mesh.shape["sx"], mesh.shape["sy"]
    return jax.shard_map(
        functools.partial(shards, n_x, n_y),
        mesh=mesh,
        in_specs=(P(None, None, "sx", "sy"), P(None, "sx", "sy"), P(), P(), P()),
        out_specs=(P(None, None, None, None, "sx", "sy"), P()),
        check_vma=False,
    )
```

```python
import functools
import jax
import jax.numpy as jnp
from jax import lax
from jax.experimental import pallas as pl
from jax.experimental.pallas import tpu as pltpu
from jax.sharding import PartitionSpec as P

NFFT = 256
LANES = 128
EPS = 1e-06
MESH = pl.DeviceIdType.MESH


def fill_twiddle(bins, nbins, tw):
    shape = (nbins, NFFT)
    row = lax.broadcasted_iota(jnp.int32, shape, 0)
    step = lax.broadcasted_iota(jnp.int32, shape, 1)
    number = jnp.zeros(shape, jnp.int32)
    for f in range(nbins):
        number = jnp.where(row == f, bins[f], number)
    turn = 2.0 * jnp.pi / NFFT
    window = 0.5 - 0.5 * jnp.cos(step.astype(jnp.float32) * turn)
    norm_c = lax.rsqrt(jnp.sum(window * window, axis=1, keepdims=True))
    phase = lax.rem(number * step, NFFT)
    angle = phase.astype(jnp.float32) * turn
    tw[:nbins, :] = norm_c * window * jnp.cos(angle)
    tw[nbins:, :] = -(norm_c * window) * jnp.sin(angle)


def shifted_rows(start, nq, length, tw):
    tile = start // LANES
    shift = start - tile * LANES
    wide = lax.broadcasted_iota(jnp.int32, (nq, LANES), 1)
    keep = wide < shift
    zero = jnp.zeros((nq, LANES), jnp.float32)
    prev, pieces = zero, []
    for j in range(NFFT // LANES):
        cur = pltpu.roll(tw[:, j * LANES:(j + 1) * LANES], shift, 1)
        pieces.append(jnp.where(keep, prev, cur))
        prev = cur
    pieces.append(jnp.where(keep, prev, zero))
    outs = []
    for j in range(length // LANES):
        out = zero
        for i, piece in enumerate(pieces):
            out = jnp.where(tile + i == j, piece, out)
        outs.append(out)
    return jnp.concatenate(outs, axis=1).astype(jnp.bfloat16)


def split2(value):
    high = value.astype(jnp.bfloat16)
    low = (value - high.astype(jnp.float32)).astype(jnp.bfloat16)
    return jnp.concatenate([high, low], axis=0)


def main_kernel(dims, starts_hbm, bins_hbm, x_hbm, quad_hbm, guess_hbm, y_ref, z_ref,
                starts, bins, x_ref, quad_ref, guess_ref, t_ref, tw, xs, xr, sq, qs,
                w_ref, acc, sqbuf, zsend, zrecv, zall, load_sems, sems):
    (length, nvar, ctile, nblock, nbins, nmode, n_x, n_y, per, grid_points) = dims
    n = n_x * n_y
    me = lax.axis_index("sx") * n_y + lax.axis_index("sy")
    per_var = ctile // nvar
    nq = 2 * nbins
    loads = [
        pltpu.make_async_copy(src, dst, load_sems.at[i])
        for i, (src, dst) in enumerate(
            [
                (bins_hbm, bins),
                (starts_hbm, starts),
                (quad_hbm, quad_ref),
                (x_hbm, x_ref),
                (guess_hbm, guess_ref),
            ]
        )
    ]
    for load in loads:
        load.start()

    ix, iy = lax.axis_index("sx"), lax.axis_index("sy")

    def each_partner(act):
        def pick(dx, dy):
            tx, ty = lax.rem(ix + dx, n_x), lax.rem(iy + dy, n_y)
            act(tx * n_y + ty, (tx, ty))

        for dy in range(1, n_y):
            pick(0, dy)

        def go(dx, carry):
            for dy in range(n_y):
                pick(dx, dy)
            return carry

        lax.fori_loop(1, n_x, go, 0, unroll=5)

    barrier = pltpu.get_barrier_semaphore()
    each_partner(
        lambda t, where: pl.semaphore_signal(
            barrier, inc=1, device_id=where, device_id_type=MESH
        )
    )

    def spread(src, dst, phase, by_target):
        each_partner(
            lambda t, where: pltpu.make_async_remote_copy(
                src_ref=src.at[t] if by_target else src,
                dst_ref=dst.at[me],
                send_sem=sems.at[2 * phase],
                recv_sem=sems.at[2 * phase + 1],
                device_id=where,
                device_id_type=MESH,
            ).start()
        )

    def wait_all(dst, sem):
        rest = dst.at[pl.ds(0, n - 1)]
        pltpu.make_async_copy(rest, rest, sems.at[sem]).wait()

    loads[0].wait()
    fill_twiddle(bins, nbins, tw)
    for load in loads[1:]:
        load.wait()
    rows = x_ref.shape[0]
    step = rows // 16

    @pl.loop(0, 16)
    def _(i):
        at = pl.ds(pl.multiple_of(i * step, step), step)
        xs[at, :] = x_ref[at, :].astype(jnp.float32)

    lane = lax.broadcasted_iota(jnp.int32, (1, LANES), 1)
    quads = [quad_ref[c // per_var, c % per_var:c % per_var + 1, :] for c in range(ctile)]
    total = jnp.zeros((1, LANES), jnp.float32)
    for c in range(ctile):
        col = xs[pl.ds(c, length, stride=ctile), :]
        xr[:, c * LANES:(c + 1) * LANES] = col.astype(jnp.bfloat16)
        sums = jnp.sum(col * col, axis=0, keepdims=True) * quads[c]
        one = jnp.sum(sums, axis=1, keepdims=True)
        total = total + jnp.where(lane == c // per_var, one, 0.0)
    sq[...] = total

    for f in range(nbins):
        g_re, g_im = guess_ref[f, 0], guess_ref[f, 1]
        w_ref[f] = split2(
            jnp.concatenate(
                [
                    jnp.concatenate([g_re, -g_im], axis=1),
                    jnp.concatenate([g_im, g_re], axis=1),
                ],
                axis=0,
            )
        )

    pl.semaphore_wait(barrier, n - 1)
    spread(sq, sqbuf, 0, False)

    @pl.loop(0, nblock // 4)
    def _(i):
        for k in range(4):
            b = i * 4 + k
            t_ref[pl.ds(pl.multiple_of(b * nq, nq), nq), :] = shifted_rows(
                starts[b], nq, length, tw
            )

    chunks = 4
    chunk = nblock * nq // chunks

    def transform(j):
        @pl.loop(0, chunks)
        def _(i):
            at = pl.ds(pl.multiple_of(i * chunk, chunk), chunk)
            out = jnp.dot(
                t_ref[at, :],
                xr[:, 2 * j * LANES:2 * (j + 1) * LANES],
                preferred_element_type=jnp.float32,
            )
            qs[2 * j, at, :] = out[:, :LANES]
            qs[2 * j + 1, at, :] = out[:, LANES:]

    def fold(value):
        return value[:2 * nmode] + value[2 * nmode:]

    def project(f, j, cols):
        for c in (2 * j, 2 * j + 1):
            for p in range(2):
                part = qs[c, pl.ds(p * nbins + f, nblock, stride=nq), :]
                y_ref[f, p * nblock:(p + 1) * nblock, c * LANES:(c + 1) * LANES] = (
                    part * cols[c]
                ).astype(jnp.bfloat16)
        y = y_ref[f, :, 2 * j * LANES:2 * (j + 1) * LANES]
        u = fold(jnp.dot(w_ref[f], y, preferred_element_type=jnp.float32))
        return fold(
            lax.dot_general(
                split2(u), y, (((1,), (1,)), ((), ())), preferred_element_type=jnp.float32
            )
        )

    pairs = ctile // 2
    for j in range(pairs):
        transform(j)

    wait_all(sqbuf, 1)
    sqbuf[me] = sq[...]
    total = jnp.sum(sqbuf[...], axis=0)
    scale = lax.rsqrt(total / (length * grid_points) + EPS)
    cols = []
    for c in range(ctile):
        one = jnp.sum(jnp.where(lane == c // per_var, scale, 0.0), axis=1, keepdims=True)
        cols.append(one * jnp.sqrt(quads[c]))

    for j in range(pairs - 1):
        for f in range(nbins):
            a = project(f, j, cols)
            acc[f] = a if j == 0 else acc[f] + a

    low_half = lax.broadcasted_iota(jnp.int32, (nmode, LANES), 1) < nblock
    parts = nmode // per
    for f in range(nbins):
        a = project(f, pairs - 1, cols)
        if pairs > 1:
            a = a + acc[f]
        a = a * (1.0 / (3.0 * grid_points))
        up = a[:nmode]
        z = pltpu.roll(a[nmode:], nblock, 1) + jnp.where(low_half, up, -up)
        for s in range(parts):
            zsend[f * parts + s] = z[s * per:(s + 1) * per]
    owners = nbins * parts
    for s in range(owners, n):
        zsend[s] = jnp.zeros((per, LANES), jnp.float32)

    spread(zsend, zrecv, 1, True)
    wait_all(zrecv, 3)
    zrecv[me] = zsend[me]
    zall[me] = jnp.sum(zrecv[...], axis=0)
    spread(zall.at[me], zall, 2, False)
    wait_all(zall, 5)
    for s in range(owners):
        z_ref[s * per:(s + 1) * per] = zall[s]
    wait_all(zrecv, 2)
    wait_all(zall, 4)
    wait_all(sqbuf, 0)


def modes_kernel(dims, y_ref, z_ref, modes_hbm, energy_ref, out, sems):
    ctile, nblock, nbins, nmode = dims
    span = 2 * nmode * ctile
    low_half = lax.broadcasted_iota(jnp.int32, (nmode, LANES), 1) < nblock
    column = lax.broadcasted_iota(jnp.int32, (nmode, nbins), 1)
    energy = jnp.zeros((nmode, nbins), jnp.float32)

    def store(f):
        at = pl.ds(f * span, span)
        return pltpu.make_async_copy(out.at[at], modes_hbm.at[at], sems.at[f])

    for f in range(nbins):
        z = z_ref[f * nmode:(f + 1) * nmode]
        norms = jnp.sum(z * z, axis=1, keepdims=True)
        energy = jnp.where(column == f, jnp.sqrt(norms / nblock), energy)
        coef = z * lax.rsqrt(norms + EPS)
        lhs = jnp.concatenate(
            [jnp.where(low_half, coef, -coef), pltpu.roll(coef, nblock, 1)], axis=0
        ).astype(jnp.bfloat16)
        m = jnp.dot(lhs, y_ref[f], preferred_element_type=jnp.float32)
        for c in range(ctile):
            out[pl.ds(f * span + c, 2 * nmode, stride=ctile), :] = (
                m[:, c * LANES:(c + 1) * LANES]
            )
        if f > 0:
            store(f - 1).start()
    energy_ref[...] = energy
    store(nbins - 1).start()
    for f in range(nbins):
        store(f).wait()


def shards(n_x, n_y, snapshots, quad_weight, mode_guess, bins, starts):
    length, nvar, cols_x, cols_y = snapshots.shape
    nbins = bins.shape[0]
    nblock = starts.shape[0]
    nmode = mode_guess.shape[-1]
    ctile = nvar * cols_x
    points = ctile * cols_y
    nq = 2 * nbins
    n = n_x * n_y
    grid_points = cols_x * cols_y * n
    vmem = pl.BlockSpec(memory_space=pltpu.VMEM)
    hbm = pl.BlockSpec(memory_space=pltpu.HBM)
    limit = 30 * 1024 * 1024

    x = snapshots.reshape(length * ctile, cols_y)
    guess = jnp.transpose(mode_guess, (0, 2, 3, 1))

    operands = [
        pltpu.with_memory_space_constraint(value, pltpu.HBM)
        for value in (starts, bins, x, quad_weight, guess)
    ]
    per = max(1, nbins * nmode // n)
    dims = (length, nvar, ctile, nblock, nbins, nmode, n_x, n_y, per, grid_points)
    y, z = pl.pallas_call(
        functools.partial(main_kernel, dims),
        name="spod",
        out_shape=(
            jax.ShapeDtypeStruct((nbins, 2 * nblock, points), jnp.bfloat16),
            jax.ShapeDtypeStruct((nbins * nmode, LANES), jnp.float32),
        ),
        in_specs=[hbm] * 5,
        out_specs=(vmem, vmem),
        scratch_shapes=[
            pltpu.SMEM(starts.shape, jnp.int32),
            pltpu.SMEM(bins.shape, jnp.int32),
            pltpu.VMEM(x.shape, jnp.bfloat16),
            pltpu.VMEM(quad_weight.shape, jnp.float32),
            pltpu.VMEM(guess.shape, jnp.float32),
            pltpu.VMEM((nblock * nq, length), jnp.bfloat16),
            pltpu.VMEM((nq, NFFT), jnp.float32),
            pltpu.VMEM((length * ctile, cols_y), jnp.float32),
            pltpu.VMEM((length, points), jnp.bfloat16),
            pltpu.VMEM((1, LANES), jnp.float32),
            pltpu.VMEM((ctile, nblock * nq, LANES), jnp.float32),
            pltpu.VMEM((nbins, 4 * nmode, 2 * nblock), jnp.bfloat16),
            pltpu.VMEM((nbins, 2 * nmode, LANES), jnp.float32),
            pltpu.VMEM((n, 1, LANES), jnp.float32),
            pltpu.VMEM((n, per, LANES), jnp.float32),
            pltpu.VMEM((n, per, LANES), jnp.float32),
            pltpu.VMEM((n, per, LANES), jnp.float32),
            pltpu.SemaphoreType.DMA((5,)),
            pltpu.SemaphoreType.DMA((6,)),
        ],
        compiler_params=pltpu.CompilerParams(
            collective_id=0, has_side_effects=True, vmem_limit_bytes=limit
        ),
    )(*operands)

    modes, energy = pl.pallas_call(
        functools.partial(modes_kernel, (ctile, nblock, nbins, nmode)),
        name="modes",
        out_shape=(
            jax.ShapeDtypeStruct((nbins * 2 * nmode * ctile, cols_y), jnp.float32),
            jax.ShapeDtypeStruct((nmode, nbins), jnp.float32),
        ),
        in_specs=[vmem, vmem],
        out_specs=(hbm, vmem),
        scratch_shapes=[
            pltpu.VMEM((nbins * 2 * nmode * ctile, cols_y), jnp.float32),
            pltpu.SemaphoreType.DMA((nbins,)),
        ],
        compiler_params=pltpu.CompilerParams(vmem_limit_bytes=limit),
    )(y, z)
    return (
        modes.reshape(nbins, 2, nmode, nvar, cols_x, cols_y),
        energy.T,
    )


def solution(mesh):
    n_x, n_y = mesh.shape["sx"], mesh.shape["sy"]
    return jax.shard_map(
        functools.partial(shards, n_x, n_y),
        mesh=mesh,
        in_specs=(P(None, None, "sx", "sy"), P(None, "sx", "sy"), P(), P(), P()),
        out_specs=(P(None, None, None, None, "sx", "sy"), P()),
        check_vma=False,
    )
```
